256 devices in a mesh: gx: 16 (over x, y_lo, core), gy: 16 (over y_hi, z).
Axes of the slice: x: 4, y: 4 (y_hi: 2, y_lo: 2; y = y_hi * 2 + y_lo), z: 8, core: 2. Of those that a mesh axis runs over, the one named last changes fastest.
Arguments:
- object_field: float32 [2, 1024, 1024], P(None, 'gy', 'gx'), may hold values from -1 to 1
- probe_modes: float32 [2, 1024, 128], P(None, ('gy', 'gx')), may hold values from -1.5 to 1.5
- positions: int32 [16, 16, 12, 2], P('gy', 'gx'), may hold values from 4 to 60, as said below
- amplitudes: float32 [16, 16, 12, 128, 128], P('gy', 'gx'), may hold values from 0 to 2
Outputs:
- object_out: float32 [2, 1024, 1024], P(None, 'gy', 'gx')
- probe_out: float32 [2, 1024, 128], P(None, ('gy', 'gx'))
The draws below stay inside these ranges and needn't reach their ends.
Inputs may be any that keep to these rules, and one draw needn't show every extreme that they name: `positions`: each entry is a (row, column) inside its own tile; the centres of one tile lie at distinct cells of the 16 grid, each moved from the cell's middle by at most 4 cells along each dimension.
All inputs are finite; a program needn't handle non-finite values.
Results may differ from the reference program's by a relative error of at most 0.00065.
The reference program's roundings to bfloat16 on the way count: a program that leaves them out, or rounds other values in their place, can miss the bound.
Values sent between devices are 32-bit elements; how exact they have to be, the bound alone decides.
No kernel may reach another device: no remote copies, remote signals or barrier semaphores. Data moves between devices by JAX's collectives and lax.ppermute only.
A program may use at most 64 MiB of HBM per device.

```python
import math
import jax
import jax.numpy as jnp
from jax import lax

PROBE = 128
MODES = 8
TILE = 64
STRIDE = 16
POS_DEV = 12
ITERS = 2
TILES_Y = 16
TILES_X = 16
NY = 1024
NX = 1024


def draw_positions(key, part):
    grid_cells = TILE // STRIDE
    tile_count = TILES_Y * TILES_X
    keys = jax.random.split(jax.random.fold_in(key, 11), tile_count)

    def one_tile(subkey):
        chosen = jax.random.permutation(subkey, grid_cells * grid_cells)[:POS_DEV]
        jitter = jax.random.randint(jax.random.fold_in(subkey, 3), (POS_DEV, 2), -4, 5)
        cells = jnp.stack([chosen // grid_cells, chosen % grid_cells], axis=1)
        return cells * STRIDE + STRIDE // 2 + jitter
    return jax.vmap(one_tile)(keys).reshape(TILES_Y, TILES_X, POS_DEV, 2).astype(jnp.int32)


def draw_object_field(key, part):
    base = jax.random.fold_in(key, 23)
    magnitude_key = jax.random.fold_in(base, 1)
    phase_key = jax.random.fold_in(base, 2)
    magnitude = jax.random.uniform(magnitude_key, (NY, NX), jnp.float32, 0.5, 1.0)
    phase = jax.random.uniform(phase_key, (NY, NX), jnp.float32, -0.6, 0.6)
    return jnp.stack([magnitude * jnp.cos(phase), magnitude * jnp.sin(phase)]).astype(jnp.float32)


def steps_of(stream_key, dims, shards, least, high):
    level = 1.0
    for position, blocks in shards:
        heights = jax.random.uniform(jax.random.fold_in(jax.random.fold_in(stream_key, 6), position), (blocks,), jnp.float32, least / len(shards), high / len(shards))
        level = level * jnp.repeat(jnp.exp(heights), dims[position] // blocks).reshape((-1,) + (1,) * (len(dims) - 1 - position))
    return level


def normal_values(rng, dims, deviation, bound, shards=(), kind=jnp.bfloat16):
    values = jax.random.normal(rng, dims, jnp.float32) * deviation
    if len(shards) > 0:
        values = steps_of(rng, dims, shards, -0.22, 0.18) * values
    return jnp.clip(values, min=-bound, max=bound).astype(kind)


def setup_inputs(seed: int = 0) -> dict:
    streams_of = jax.random.split(jax.random.key(seed), 5)
    return {
        "object_field": draw_object_field(jax.random.fold_in(streams_of[4], 71), 0),
        "probe_modes": normal_values(streams_of[1], (2, MODES * PROBE, PROBE), 0.25, 1.5, ((1, 256),), jnp.float32),
        "positions": draw_positions(jax.random.fold_in(streams_of[4], 71), 0),
        "amplitudes": jnp.clip(2.0 * jax.random.uniform(streams_of[3], (TILES_Y, TILES_X, POS_DEV, PROBE, PROBE), jnp.float32) ** steps_of(streams_of[3], (TILES_Y, TILES_X, POS_DEV, PROBE, PROBE), ((0, 16), (1, 16)), -0.2, 0.2), 0.0, 2.0),
    }


SOFT_FLOOR = 0.05
OBJECT_REG = 1.0
PROBE_REG = 1.0

def tables(probe_side, sign_flip):
    indices = jnp.arange(probe_side, dtype=jnp.int32)
    phases = indices[:, None] * indices[None, :] % probe_side
    angles = phases.astype(jnp.float32) * (2.0 * math.pi / probe_side)
    factor = 1.0 / math.sqrt(probe_side)
    cosine = jnp.cos(angles) * factor
    sine_part = sign_flip * jnp.sin(angles) * factor
    left_op = jnp.stack([jnp.stack([cosine, -sine_part]), jnp.stack([sine_part, cosine])]).transpose(0, 2, 1, 3)
    right_op = jnp.stack([jnp.stack([cosine, sine_part]), jnp.stack([-sine_part, cosine])]).transpose(0, 2, 1, 3)
    return (left_op.astype(jnp.bfloat16), right_op.astype(jnp.bfloat16))

def transform(signal, operators):
    left_op, right_op = operators
    signal = lax.optimization_barrier(signal)
    halfway = jnp.einsum('dpcr,crmq->dpmq', left_op.astype(jnp.float32), signal.astype(jnp.float32), precision=lax.Precision.HIGHEST).astype(jnp.bfloat16)
    halfway = lax.optimization_barrier(halfway)
    return jnp.einsum('crmq,cqdk->drmk', halfway.astype(jnp.float32), right_op.astype(jnp.float32), precision=lax.Precision.HIGHEST)

def position_terms(patch_obj, probe, measured, forward, inverse):
    obj_real = patch_obj[0][:, None, :]
    obj_imag = patch_obj[1][:, None, :]
    wave_real = probe[0] * obj_real - probe[1] * obj_imag
    wave_imag = probe[0] * obj_imag + probe[1] * obj_real
    signal = jnp.stack([wave_real, wave_imag]).astype(jnp.bfloat16)
    spectrum = transform(signal, forward)
    intensity = lax.optimization_barrier(jnp.sum(spectrum[0] * spectrum[0] + spectrum[1] * spectrum[1], axis=1))
    shrink = 1.0 - measured / jnp.sqrt(intensity + SOFT_FLOOR)
    residual = (spectrum * shrink[None, :, None, :]).astype(jnp.bfloat16)
    change = transform(residual, inverse)
    grad_real = lax.optimization_barrier(jnp.sum(probe[0] * change[0] + probe[1] * change[1], axis=1))
    grad_imag = lax.optimization_barrier(jnp.sum(probe[0] * change[1] - probe[1] * change[0], axis=1))
    probe_real = obj_real * change[0] + obj_imag * change[1]
    probe_imag = obj_real * change[1] - obj_imag * change[0]
    weight_probe = patch_obj[0] * patch_obj[0] + patch_obj[1] * patch_obj[1]
    return (jnp.stack([grad_real, grad_imag]), jnp.stack([probe_real, probe_imag]), weight_probe)

def reference(object_field, probe_modes, positions, amplitudes):
    margin = PROBE // 2
    forward = tables(PROBE, -1.0)
    inverse = tables(PROBE, 1.0)
    tile_rows = jnp.arange(TILES_Y, dtype=jnp.int32)[:, None, None] * TILE
    tile_cols = jnp.arange(TILES_X, dtype=jnp.int32)[None, :, None] * TILE
    row_list = (positions[..., 0] + tile_rows).reshape(-1).astype(jnp.int32)
    col_list = (positions[..., 1] + tile_cols).reshape(-1).astype(jnp.int32)
    measured_all = amplitudes.reshape(-1, PROBE, PROBE)
    probe = probe_modes.reshape(2, MODES, PROBE, PROBE).transpose(0, 2, 1, 3)
    current = object_field
    for iteration in range(ITERS):
        padded = jnp.pad(current, ((0, 0), (margin, margin), (margin, margin)))
        weight_obj = lax.optimization_barrier(jnp.sum(probe[0] * probe[0] + probe[1] * probe[1], axis=1))

        def visit(running, visit_item):
            grad_obj, grad_probe, weight_probe = running
            row_at, col_at, measured = visit_item
            zero_index = jnp.int32(0)
            patch_obj = lax.dynamic_slice(padded, (zero_index, row_at, col_at), (2, PROBE, PROBE))
            g_obj, g_probe, w_probe = position_terms(patch_obj, probe, measured, forward, inverse)
            stacked = jnp.concatenate([g_obj, weight_obj[None]], axis=0)
            before = lax.dynamic_slice(grad_obj, (zero_index, row_at, col_at), (3, PROBE, PROBE))
            grad_obj = lax.dynamic_update_slice(grad_obj, before + stacked, (zero_index, row_at, col_at))
            return ((grad_obj, grad_probe + g_probe, weight_probe + w_probe), None)
        initial = (jnp.zeros((3, NY + PROBE, NX + PROBE), jnp.float32), jnp.zeros((2, PROBE, MODES, PROBE), jnp.float32), jnp.zeros((PROBE, PROBE), jnp.float32))
        (grad_obj, grad_probe, weight_probe), _ = lax.scan(visit, initial, (row_list, col_list, measured_all))
        inner = grad_obj[:, margin:margin + NY, margin:margin + NX]
        new_object = current - inner[0:2] / (inner[2] + OBJECT_REG)
        probe = probe - grad_probe / (weight_probe[:, None, :] + PROBE_REG)
        current = new_object
    return (current, probe.transpose(0, 2, 1, 3).reshape(2, MODES * PROBE, PROBE))
```

```python
import math

import jax
import jax.numpy as jnp
import numpy as np
from jax import lax
from jax.experimental import pallas as pl
from jax.experimental.pallas import tpu as pltpu
from jax.sharding import PartitionSpec as P

MODES = 8
ITERS = 2
SOFT_FLOOR = 0.05
OBJECT_REG = 1.0
PROBE_REG = 1.0

BAND = 32
DEVICES = 256
CORE = 1
Y_FAR, Y_NEAR = 0b10000010, 0b00000010
X_FAR, X_NEAR = 0b00001100, 0b00000100
Z_STEPS = (0b00010000, 0b00100000, 0b01100000)
PLANE_STEPS = ((Y_FAR, X_FAR), (Y_NEAR, X_NEAR), (X_FAR, Y_FAR), (X_NEAR, Y_NEAR))


def mesh_place(device):
    return (device % 16) * 16 + device // 16


def exchange(block, flips):
    if isinstance(flips, int):
        flips = (flips, flips)
    pairs = [(d, d ^ flips[d & 1]) for d in range(DEVICES)]
    return lax.ppermute(block, ("gx", "gy"), [(mesh_place(a), mesh_place(b)) for a, b in pairs])


def table(side):
    index = np.arange(side)
    angle = (index[:, None] * index[None, :] % side).astype(np.float32) * np.float32(2.0 * math.pi / side)
    factor = np.float32(1.0 / math.sqrt(side))
    real = (np.cos(angle) * factor).astype(jnp.bfloat16)
    imag = (-np.sin(angle) * factor).astype(jnp.bfloat16)
    return np.block([[real, -imag], [imag, real]])


def aligned(row):
    return pl.multiple_of(row - lax.rem(row, 8), 8)


def gray(delta):
    return lax.bitwise_xor(delta, lax.shift_right_logical(delta, 1))


def groups(spot_ref):
    for x in range(4):
        for y in range(4):
            far_x, far_y = gray(lax.bitwise_xor(spot_ref[1], x)), gray(lax.bitwise_xor(spot_ref[2], y))
            yield (y // 2) * 64 + x * 2 + y % 2, far_y * 4 + far_x, far_x * 4 + far_y


def sweep_kernel(
    pos_ref, spot_ref, ext_ref, mine_ref, other_ref, amp_ref, a_ref, b_ref,
    keep_ref, send_ref, top_ref, middle_ref, bottom_ref,
    probe_s, grad_s, obj_s, wp_s, patch_s, weight_s, half_s, miss_s, back_s,
):
    count, side = amp_ref.shape[0], amp_ref.shape[1]
    bands = side // BAND
    wide = 2 * side
    on_zero = spot_ref[0] == 0
    upper = lax.broadcasted_iota(jnp.int32, (8, side), 0) < 4

    def joined(first, second):
        return jnp.where(upper, first, pltpu.roll(second, 4, 0)), jnp.where(upper, pltpu.roll(first, 4, 0), second)

    for pair, place_0, place_1 in groups(spot_ref):
        for z in range(8):
            tile_0 = jnp.where(on_zero, mine_ref[place_0, z], other_ref[place_0, z])
            tile_1 = jnp.where(on_zero, other_ref[place_1, z], mine_ref[place_1, z])
            rows = pl.ds((pair + z * 8) * 8, 8)
            probe_s[0, rows, :], probe_s[1, rows, :] = joined(tile_0, tile_1)

    obj_s[...] = jnp.zeros_like(obj_s)
    grad_s[...] = jnp.zeros_like(grad_s)
    wp_s[...] = jnp.zeros_like(wp_s)
    weight = jnp.zeros((side, side), jnp.float32)
    for m in range(MODES):
        for c in range(2):
            p = probe_s[c, pl.ds(m * side, side), :]
            weight = weight + p * p
    weight_s[...] = weight

    def fetch(i, slot):
        row, col = pos_ref[i, 0], pos_ref[i, 1]
        for c in range(2):
            rows = ext_ref[c, pl.ds(aligned(row), side + 8), :]
            rows = pltpu.roll(rows, wide - col, 1)[:, :side]
            patch_s[slot, c] = pltpu.roll(rows, side + 8 - lax.rem(row, 8), 0)[:side]
        wp_s[...] += patch_s[slot, 0] * patch_s[slot, 0] + patch_s[slot, 1] * patch_s[slot, 1]

    def forward_rows(slot, j):
        real, imag = [], []
        for m in (2 * j, 2 * j + 1):
            p_re = probe_s[0, pl.ds(m * side, side), :]
            p_im = probe_s[1, pl.ds(m * side, side), :]
            o_re, o_im = patch_s[slot, 0], patch_s[slot, 1]
            real.append((p_re * o_re - p_im * o_im).astype(jnp.bfloat16))
            imag.append((p_re * o_im + p_im * o_re).astype(jnp.bfloat16))
        psi = jnp.concatenate([jnp.concatenate(real, 1), jnp.concatenate(imag, 1)], 0)
        half = jnp.dot(a_ref[...], psi, preferred_element_type=jnp.float32).astype(jnp.bfloat16)
        for k in range(2):
            lanes = slice(k * side, (k + 1) * side)
            half_s[2 * j + k] = jnp.concatenate([half[:side, lanes], half[side:, lanes]], 1)

    def forward_cols(i, b):
        rows = slice(b * BAND, (b + 1) * BAND)
        half = half_s[:, rows, :].reshape(MODES * BAND, wide)
        far = jnp.dot(half, b_ref[...], preferred_element_type=jnp.float32).reshape(MODES, BAND, wide)
        power = jnp.sum(far * far, axis=0)
        power = power[:, :side] + power[:, side:]
        shrink = 1.0 - amp_ref[i, rows, :] * lax.rsqrt(power + SOFT_FLOOR)
        shrink = jnp.concatenate([shrink, shrink], 1)
        for m in range(MODES):
            miss = (far[m] * shrink).astype(jnp.bfloat16)
            miss_s[pl.ds(b * BAND, BAND), pl.ds(m * side, side)] = miss[:, :side]
            miss_s[pl.ds(side + b * BAND, BAND), pl.ds(m * side, side)] = miss[:, side:]

    def inverse_rows(j):
        miss = miss_s[:, pl.ds(j * wide, wide)]
        back = jnp.dot(b_ref[...], miss, preferred_element_type=jnp.float32).astype(jnp.bfloat16)
        for k in range(2):
            lanes = slice(k * side, (k + 1) * side)
            back_s[2 * j + k] = jnp.concatenate([back[:side, lanes], back[side:, lanes]], 1)

    def inverse_cols(i, slot, b):
        row, col = pos_ref[i, 0], pos_ref[i, 1]
        rows = slice(b * BAND, (b + 1) * BAND)
        back = back_s[:, rows, :].reshape(MODES * BAND, wide)
        delta = jnp.dot(back, a_ref[...], preferred_element_type=jnp.float32).reshape(MODES, BAND, wide)
        o_re, o_im = patch_s[slot, 0, rows, :], patch_s[slot, 1, rows, :]
        g_re = jnp.zeros((BAND, side), jnp.float32)
        g_im = jnp.zeros((BAND, side), jnp.float32)
        for m in range(MODES):
            span = pl.ds(m * side + b * BAND, BAND)
            d_re, d_im = delta[m, :, :side], delta[m, :, side:]
            p_re, p_im = probe_s[0, span, :], probe_s[1, span, :]
            g_re += p_re * d_re + p_im * d_im
            g_im += p_re * d_im - p_im * d_re
            grad_s[0, span, :] += o_re * d_re + o_im * d_im
            grad_s[1, span, :] += o_re * d_im - o_im * d_re
        for c, part in enumerate((g_re, g_im, weight_s[rows, :])):
            part = jnp.concatenate([part, jnp.zeros((8, side), jnp.float32)], 0)
            part = pltpu.roll(part, lax.rem(row, 8), 0)
            placed = pltpu.roll(jnp.concatenate([part, jnp.zeros_like(part)], 1), col, 1)
            obj_s[c, pl.ds(aligned(row) + b * BAND, BAND + 8), :] += placed

    fetch(0, 0)
    for j in range(MODES // 2):
        forward_rows(0, j)
    for b in range(bands):
        forward_cols(0, b)

    def step(i, carry):
        slot = lax.rem(i, 2)
        fetch(i + 1, 1 - slot)
        for j in range(MODES // 2):
            inverse_rows(j)
            forward_rows(1 - slot, j)
        for b in range(bands):
            inverse_cols(i, slot, b)
            forward_cols(i + 1, b)
        return carry

    lax.fori_loop(0, count - 1, step, 0)
    last = count - 1
    for j in range(MODES // 2):
        inverse_rows(j)
    for b in range(bands):
        inverse_cols(last, last % 2, b)

    tile = side // 2
    top_ref[...] = obj_s[:, :tile, :]
    middle_ref[...] = obj_s[:, tile : 2 * tile, :]
    bottom_ref[...] = obj_s[:, 2 * tile :, :]
    for pair, place_0, place_1 in groups(spot_ref):
        place_mine = jnp.where(on_zero, place_0, place_1)
        place_other = jnp.where(on_zero, place_1, place_0)
        for slot in range(9):
            if slot < 8:
                rows = pl.ds((pair + slot * 8) * 8, 8)
                tile_0, tile_1 = joined(grad_s[0, rows, :], grad_s[1, rows, :])
            else:
                start = (pair % 8) * 8
                tile_0, tile_1 = joined(wp_s[pl.ds(start, 8), :], wp_s[pl.ds(start + side // 2, 8), :])
            keep_ref[place_mine, slot] = jnp.where(on_zero, tile_0, tile_1)
            send_ref[place_other, slot] = jnp.where(on_zero, tile_1, tile_0)


def sweep(centres, spot, extended, mine, other, measured, left_op, right_op):
    count, side = measured.shape[0], measured.shape[1]
    tile, wide, extent = side // 2, 2 * side, extended.shape[1]
    rows = MODES * side
    vmem = pl.BlockSpec(memory_space=pltpu.VMEM)
    smem = pl.BlockSpec(memory_space=pltpu.SMEM)
    f32, bf16 = jnp.float32, jnp.bfloat16
    half_sum = jax.ShapeDtypeStruct((16, 9, 8, side), f32)
    strip = jax.ShapeDtypeStruct((3, tile, wide), f32)
    return pl.pallas_call(
        sweep_kernel,
        in_specs=[smem, smem] + [vmem] * 6,
        out_specs=[vmem] * 5,
        out_shape=[half_sum, half_sum, strip, strip, strip],
        scratch_shapes=[
            pltpu.VMEM((2, rows, side), f32),
            pltpu.VMEM((2, rows, side), f32),
            pltpu.VMEM((3, extent, wide), f32),
            pltpu.VMEM((side, side), f32),
            pltpu.VMEM((2, 2, side, side), f32),
            pltpu.VMEM((side, side), f32),
            pltpu.VMEM((MODES, side, wide), bf16),
            pltpu.VMEM((wide, rows), bf16),
            pltpu.VMEM((MODES, side, wide), bf16),
        ],
        compiler_params=pltpu.CompilerParams(vmem_limit_bytes=32 << 20),
        cost_estimate=pl.CostEstimate(
            flops=count * 4 * 2 * wide * wide * rows, bytes_accessed=8 << 20, transcendentals=0
        ),
        name="sweep",
    )(centres, spot, extended, mine, other, measured, left_op, right_op)


def shifted(block, axis, distance):
    devices = range(lax.axis_size(axis))
    return lax.ppermute(block, axis, [(i - distance, i) for i in devices if i - distance in devices])


def extended_2(tile):
    side = tile.shape[1]
    above, below = shifted(tile, "gy", 1), shifted(tile, "gy", -1)
    tall = jnp.concatenate([above, tile, below], axis=1)
    before, after = shifted(tall, "gx", 1), shifted(tall, "gx", -1)
    blank = jnp.zeros((2, 3 * side, side), jnp.float32)
    return jnp.concatenate([before, tall, after, blank], axis=2)


def folded(top, middle, bottom):
    side = middle.shape[1]
    strip = middle + shifted(bottom, "gy", 1) + shifted(top, "gy", -1)
    before = shifted(strip[:, :, 2 * side : 3 * side], "gx", 1)
    after = shifted(strip[:, :, :side], "gx", -1)
    return strip[:, :, side : 2 * side] + before + after


def summed_over_z(block):
    for flip in Z_STEPS:
        block = block + exchange(block, flip)
    return block


def summed(keep, send):
    block = keep + exchange(send, CORE)
    for flips in PLANE_STEPS:
        half = block.shape[0] // 2
        block = block[:half] + exchange(block[half:], flips)
    return summed_over_z(block[0])


def gathered(block):
    block = block[None]
    for flips in reversed(PLANE_STEPS):
        block = jnp.concatenate([block, exchange(block, flips)], axis=0)
    return block, exchange(block, CORE)


def local(object_field, probe_modes, positions, amplitudes):
    side = amplitudes.shape[-1]
    centres = positions.reshape(-1, 2)
    measured = amplitudes.reshape(-1, side, side)
    left_op = table(side)
    left_op, right_op = jnp.asarray(left_op), jnp.asarray(left_op.T)
    gx, gy = lax.axis_index("gx"), lax.axis_index("gy")
    z = gy % 8
    spot = jnp.stack([gx % 2, gx // 4, (gy // 8) * 2 + (gx // 2) % 2]).astype(jnp.int32)

    own = probe_modes.reshape(1, 8, side)
    own = lax.dynamic_update_slice(jnp.zeros((8, 8, side), jnp.float32), own, (z, 0, 0))
    own = summed_over_z(own)
    current = object_field
    for iteration in range(ITERS):
        mine, other = gathered(own)
        extended = extended_2(current)
        keep, send, top, middle, bottom = sweep(
            centres, spot, extended, mine, other, measured, left_op, right_op
        )
        total = summed(keep, send)
        sums = folded(top, middle, bottom)
        current = current - sums[0:2] / (sums[2] + OBJECT_REG)
        weight = total[8].reshape(2, 1, 4, side)
        weight = jnp.broadcast_to(weight, (2, 2, 4, side)).reshape(1, 2, 8, side)
        change = total[:8].reshape(4, 2, 8, side) / (weight + PROBE_REG)
        own = own - change.reshape(8, 8, side)
    own = lax.dynamic_slice(own, (z, 0, 0), (1, 8, side))
    return (current, own.reshape(2, 4, side))


def solution(mesh):
    return jax.shard_map(
        local,
        mesh=mesh,
        in_specs=(
            P(None, "gy", "gx"),
            P(None, ("gy", "gx"), None),
            P("gy", "gx", None, None),
            P("gy", "gx", None, None, None),
        ),
        out_specs=(P(None, "gy", "gx"), P(None, ("gy", "gx"), None)),
        check_vma=False,
    )
```

```python
import math

import jax
import jax.numpy as jnp
import numpy as np
from jax import lax
from jax.experimental import pallas as pl
from jax.experimental.pallas import tpu as pltpu
from jax.sharding import PartitionSpec as P

MODES = 8
ITERS = 2
SOFT_FLOOR = 0.05
OBJECT_REG = 1.0
PROBE_REG = 1.0

BAND = 32
DEVICES = 256
Y_FAR, Y_NEAR = 0b10000010, 0b00000010
X_FAR, X_NEAR = 0b00001100, 0b00000100
PLANE_STEPS = ((Y_FAR, X_FAR), (Y_NEAR, X_NEAR), (X_FAR, Y_FAR), (X_NEAR, Y_NEAR))


def mesh_place(device):
    return (device % 16) * 16 + device // 16


def exchange(block, partner):
    pairs = [(mesh_place(d), mesh_place(partner(d))) for d in range(DEVICES)]
    return lax.ppermute(block, ("gx", "gy"), pairs)


def other_core(block):
    return exchange(block, lambda d: d ^ 1)


def plane_partner(block, step):
    return exchange(block, lambda d: d ^ PLANE_STEPS[step][d & 1])


def z_even_pair(block):
    return exchange(block, lambda d: d ^ 16)


def z_odd_pair(block):
    def partner(d):
        z = d >> 4 & 7
        return d & ~112 | (z + (1 if z % 2 else -1)) % 8 << 4

    return exchange(block, partner)


def table(side):
    index = np.arange(side)
    angle = (index[:, None] * index[None, :] % side).astype(np.float32) * np.float32(2.0 * math.pi / side)
    factor = np.float32(1.0 / math.sqrt(side))
    real = (np.cos(angle) * factor).astype(jnp.bfloat16)
    imag = (-np.sin(angle) * factor).astype(jnp.bfloat16)
    return np.block([[real, -imag], [imag, real]])


def aligned(row):
    return pl.multiple_of(row - lax.rem(row, 8), 8)


def gray(delta):
    return lax.bitwise_xor(delta, lax.shift_right_logical(delta, 1))


def groups(spot_ref):
    for x in range(4):
        for y in range(4):
            far_x, far_y = gray(lax.bitwise_xor(spot_ref[1], x)), gray(lax.bitwise_xor(spot_ref[2], y))
            yield (y // 2) * 64 + x * 2 + y % 2, far_y * 4 + far_x, far_x * 4 + far_y


def sweep_kernel(
    pos_ref, spot_ref, ext_ref, mine_ref, other_ref, amp_ref, a_ref, b_ref,
    keep_ref, send_ref, top_ref, middle_ref, bottom_ref,
    probe_s, grad_s, obj_s, wp_s, patch_s, weight_s, half_s, miss_s, back_s,
):
    count, side = amp_ref.shape[0], amp_ref.shape[1]
    bands = side // BAND
    wide = 2 * side
    on_zero = spot_ref[0] == 0
    upper = lax.broadcasted_iota(jnp.int32, (8, side), 0) < 4

    def joined(first, second):
        return jnp.where(upper, first, pltpu.roll(second, 4, 0)), jnp.where(upper, pltpu.roll(first, 4, 0), second)

    for pair, place_0, place_1 in groups(spot_ref):
        for z in range(8):
            tile_0 = jnp.where(on_zero, mine_ref[place_0, z], other_ref[place_0, z])
            tile_1 = jnp.where(on_zero, other_ref[place_1, z], mine_ref[place_1, z])
            rows = pl.ds((pair + z * 8) * 8, 8)
            probe_s[0, rows, :], probe_s[1, rows, :] = joined(tile_0, tile_1)

    obj_s[...] = jnp.zeros_like(obj_s)
    grad_s[...] = jnp.zeros_like(grad_s)
    wp_s[...] = jnp.zeros_like(wp_s)
    weight = jnp.zeros((side, side), jnp.float32)
    for m in range(MODES):
        for c in range(2):
            p = probe_s[c, pl.ds(m * side, side), :]
            weight = weight + p * p
    weight_s[...] = weight

    def fetch(i, slot):
        row, col = pos_ref[i, 0], pos_ref[i, 1]
        for c in range(2):
            rows = ext_ref[c, pl.ds(aligned(row), side + 8), :]
            rows = pltpu.roll(rows, wide - col, 1)[:, :side]
            patch_s[slot, c] = pltpu.roll(rows, side + 8 - lax.rem(row, 8), 0)[:side]
        wp_s[...] += patch_s[slot, 0] * patch_s[slot, 0] + patch_s[slot, 1] * patch_s[slot, 1]

    def forward_rows(slot, j):
        real, imag = [], []
        for m in (2 * j, 2 * j + 1):
            p_re = probe_s[0, pl.ds(m * side, side), :]
            p_im = probe_s[1, pl.ds(m * side, side), :]
            o_re, o_im = patch_s[slot, 0], patch_s[slot, 1]
            real.append((p_re * o_re - p_im * o_im).astype(jnp.bfloat16))
            imag.append((p_re * o_im + p_im * o_re).astype(jnp.bfloat16))
        psi = jnp.concatenate([jnp.concatenate(real, 1), jnp.concatenate(imag, 1)], 0)
        half = jnp.dot(a_ref[...], psi, preferred_element_type=jnp.float32).astype(jnp.bfloat16)
        for k in range(2):
            lanes = slice(k * side, (k + 1) * side)
            half_s[2 * j + k] = jnp.concatenate([half[:side, lanes], half[side:, lanes]], 1)

    def forward_cols(i, b):
        rows = slice(b * BAND, (b + 1) * BAND)
        half = half_s[:, rows, :].reshape(MODES * BAND, wide)
        far = jnp.dot(half, b_ref[...], preferred_element_type=jnp.float32).reshape(MODES, BAND, wide)
        power = jnp.sum(far * far, axis=0)
        power = power[:, :side] + power[:, side:]
        shrink = 1.0 - amp_ref[i, rows, :] * lax.rsqrt(power + SOFT_FLOOR)
        shrink = jnp.concatenate([shrink, shrink], 1)
        for m in range(MODES):
            miss = (far[m] * shrink).astype(jnp.bfloat16)
            miss_s[pl.ds(b * BAND, BAND), pl.ds(m * side, side)] = miss[:, :side]
            miss_s[pl.ds(side + b * BAND, BAND), pl.ds(m * side, side)] = miss[:, side:]

    def inverse_rows(j):
        miss = miss_s[:, pl.ds(j * wide, wide)]
        back = jnp.dot(b_ref[...], miss, preferred_element_type=jnp.float32).astype(jnp.bfloat16)
        for k in range(2):
            lanes = slice(k * side, (k + 1) * side)
            back_s[2 * j + k] = jnp.concatenate([back[:side, lanes], back[side:, lanes]], 1)

    def inverse_cols(i, slot, b):
        row, col = pos_ref[i, 0], pos_ref[i, 1]
        rows = slice(b * BAND, (b + 1) * BAND)
        back = back_s[:, rows, :].reshape(MODES * BAND, wide)
        delta = jnp.dot(back, a_ref[...], preferred_element_type=jnp.float32).reshape(MODES, BAND, wide)
        o_re, o_im = patch_s[slot, 0, rows, :], patch_s[slot, 1, rows, :]
        g_re = jnp.zeros((BAND, side), jnp.float32)
        g_im = jnp.zeros((BAND, side), jnp.float32)
        for m in range(MODES):
            span = pl.ds(m * side + b * BAND, BAND)
            d_re, d_im = delta[m, :, :side], delta[m, :, side:]
            p_re, p_im = probe_s[0, span, :], probe_s[1, span, :]
            g_re += p_re * d_re + p_im * d_im
            g_im += p_re * d_im - p_im * d_re
            grad_s[0, span, :] += o_re * d_re + o_im * d_im
            grad_s[1, span, :] += o_re * d_im - o_im * d_re
        for c, part in enumerate((g_re, g_im, weight_s[rows, :])):
            part = jnp.concatenate([part, jnp.zeros((8, side), jnp.float32)], 0)
            part = pltpu.roll(part, lax.rem(row, 8), 0)
            placed = pltpu.roll(jnp.concatenate([part, jnp.zeros_like(part)], 1), col, 1)
            obj_s[c, pl.ds(aligned(row) + b * BAND, BAND + 8), :] += placed

    fetch(0, 0)
    for j in range(MODES // 2):
        forward_rows(0, j)
    for b in range(bands):
        forward_cols(0, b)

    def step(i, carry):
        slot = lax.rem(i, 2)
        fetch(i + 1, 1 - slot)
        for j in range(MODES // 2):
            inverse_rows(j)
            forward_rows(1 - slot, j)
        for b in range(bands):
            inverse_cols(i, slot, b)
            forward_cols(i + 1, b)
        return carry

    lax.fori_loop(0, count - 1, step, 0)
    last = count - 1
    for j in range(MODES // 2):
        inverse_rows(j)
    for b in range(bands):
        inverse_cols(last, last % 2, b)

    tile = side // 2
    top_ref[...] = obj_s[:, :tile, :]
    middle_ref[...] = obj_s[:, tile : 2 * tile, :]
    bottom_ref[...] = obj_s[:, 2 * tile :, :]
    for pair, place_0, place_1 in groups(spot_ref):
        place_mine = jnp.where(on_zero, place_0, place_1)
        place_other = jnp.where(on_zero, place_1, place_0)
        for slot in range(9):
            if slot < 8:
                rows = pl.ds((pair + slot * 8) * 8, 8)
                tile_0, tile_1 = joined(grad_s[0, rows, :], grad_s[1, rows, :])
            else:
                start = (pair % 8) * 8
                tile_0, tile_1 = joined(wp_s[pl.ds(start, 8), :], wp_s[pl.ds(start + side // 2, 8), :])
            keep_ref[place_mine, slot] = jnp.where(on_zero, tile_0, tile_1)
            send_ref[place_other, slot] = jnp.where(on_zero, tile_1, tile_0)


def sweep(centres, spot, extended, mine, other, measured, left_op, right_op):
    count, side = measured.shape[0], measured.shape[1]
    tile, wide, extent = side // 2, 2 * side, extended.shape[1]
    rows = MODES * side
    vmem = pl.BlockSpec(memory_space=pltpu.VMEM)
    smem = pl.BlockSpec(memory_space=pltpu.SMEM)
    f32, bf16 = jnp.float32, jnp.bfloat16
    half_sum = jax.ShapeDtypeStruct((16, 9, 8, side), f32)
    strip = jax.ShapeDtypeStruct((3, tile, wide), f32)
    return pl.pallas_call(
        sweep_kernel,
        in_specs=[smem, smem] + [vmem] * 6,
        out_specs=[vmem] * 5,
        out_shape=[half_sum, half_sum, strip, strip, strip],
        scratch_shapes=[
            pltpu.VMEM((2, rows, side), f32),
            pltpu.VMEM((2, rows, side), f32),
            pltpu.VMEM((3, extent, wide), f32),
            pltpu.VMEM((side, side), f32),
            pltpu.VMEM((2, 2, side, side), f32),
            pltpu.VMEM((side, side), f32),
            pltpu.VMEM((MODES, side, wide), bf16),
            pltpu.VMEM((wide, rows), bf16),
            pltpu.VMEM((MODES, side, wide), bf16),
        ],
        compiler_params=pltpu.CompilerParams(vmem_limit_bytes=32 << 20),
        cost_estimate=pl.CostEstimate(
            flops=count * 4 * 2 * wide * wide * rows, bytes_accessed=8 << 20, transcendentals=0
        ),
        name="sweep",
    )(centres, spot, extended, mine, other, measured, left_op, right_op)


def shifted(block, axis, distance):
    devices = range(lax.axis_size(axis))
    return lax.ppermute(block, axis, [(i - distance, i) for i in devices if i - distance in devices])


def tall_of(tile):
    return jnp.concatenate([shifted(tile, "gy", 1), tile, shifted(tile, "gy", -1)], axis=1)


def wide_of(tall):
    side = tall.shape[2]
    before, after = shifted(tall, "gx", 1), shifted(tall, "gx", -1)
    blank = jnp.zeros((2, 3 * side, side), jnp.float32)
    return jnp.concatenate([before, tall, after, blank], axis=2)


def folded_rows(top, middle, bottom):
    return middle + shifted(bottom, "gy", 1) + shifted(top, "gy", -1)


def folded_cols(strip):
    side = strip.shape[1]
    before = shifted(strip[:, :, 2 * side : 3 * side], "gx", 1)
    after = shifted(strip[:, :, :side], "gx", -1)
    return strip[:, :, side : 2 * side] + before + after


def halved(block, step):
    half = block.shape[0] // 2
    return block[:half] + plane_partner(block[half:], step)


def doubled(block, step):
    return jnp.concatenate([block, plane_partner(block, step)], axis=0)


together = lax.optimization_barrier


def local(object_field, probe_modes, positions, amplitudes):
    side = amplitudes.shape[-1]
    centres = positions.reshape(-1, 2)
    measured = amplitudes.reshape(-1, side, side)
    left_op = table(side)
    left_op, right_op = jnp.asarray(left_op), jnp.asarray(left_op.T)
    gx, gy = lax.axis_index("gx"), lax.axis_index("gy")
    z = lax.bitwise_and(gy, 7)
    y = lax.bitwise_and(lax.shift_right_logical(gy, 2), 2) + lax.bitwise_and(lax.shift_right_logical(gx, 1), 1)
    spot = jnp.stack([lax.bitwise_and(gx, 1), lax.shift_right_logical(gx, 2), y]).astype(jnp.int32)
    is_own = (jnp.arange(8) == z)[:, None, None]

    current = object_field
    own = jnp.where(is_own, probe_modes.reshape(1, 8, side), 0.0)
    first = own + z_even_pair(own)
    second = z_odd_pair(first)
    tall = tall_of(current)
    third = z_even_pair(second)
    third, tall = together((third, tall))
    fourth = z_odd_pair(third)
    own = (first + second) + (third + fourth)
    extended = wide_of(tall)
    mine = doubled(own[None], 3)
    mine = doubled(mine, 2)
    mine, extended = together((mine, extended))
    mine = doubled(doubled(mine, 1), 0)

    for iteration in range(ITERS):
        other = other_core(mine)
        keep, send, top, middle, bottom = sweep(
            centres, spot, extended, mine, other, measured, left_op, right_op
        )
        block = keep + other_core(send)
        block, top, middle, bottom = together((block, top, middle, bottom))
        block = halved(block, 0)
        strip = folded_rows(top, middle, bottom)
        block = halved(block, 1)
        block, strip = together((block, strip))
        block = halved(block, 2)
        sums = folded_cols(strip)
        block = halved(block, 3)[0]
        block, sums = together((block, sums))
        first = block + z_even_pair(block)
        current = current - sums[0:2] / (sums[2] + OBJECT_REG)
        if iteration < ITERS - 1:
            tall = tall_of(current)
        second = z_odd_pair(first)
        if iteration < ITERS - 1:
            second, tall = together((second, tall))
            extended = wide_of(tall)
        third = z_even_pair(second)
        if iteration < ITERS - 1:
            third, extended = together((third, extended))
        fourth = z_odd_pair(third)
        total = (first + second) + (third + fourth)
        weight = total[8].reshape(2, 1, 4, side)
        weight = jnp.broadcast_to(weight, (2, 2, 4, side)).reshape(1, 2, 8, side)
        change = total[:8].reshape(4, 2, 8, side) / (weight + PROBE_REG)
        own = own - change.reshape(8, 8, side)
        if iteration < ITERS - 1:
            mine = own[None]
            for step in (3, 2, 1, 0):
                mine = doubled(mine, step)
    probe_rows = jnp.sum(jnp.where(is_own, own, 0.0), axis=0)
    return (current, probe_rows.reshape(2, 4, side))


def solution(mesh):
    return jax.shard_map(
        local,
        mesh=mesh,
        in_specs=(
            P(None, "gy", "gx"),
            P(None, ("gy", "gx"), None),
            P("gy", "gx", None, None),
            P("gy", "gx", None, None, None),
        ),
        out_specs=(P(None, "gy", "gx"), P(None, ("gy", "gx"), None)),
        check_vma=False,
    )
```
